32 devices in a mesh: group: 2 (over y), member: 4 (over z), strip: 2 (over x), sub: 2 (over core).
Axes of the slice: x: 2, y: 2, z: 4, core: 2. Of those that a mesh axis runs over, the one named last changes fastest.
Arguments:
- noisy: bfloat16 [8, 128, 128, 256], P(('group', 'member'), None, 'strip', 'sub'), parts along dimension 0, may hold values from -6 to 6
- condition: bfloat16 [24, 128, 256], P('group', ('strip', 'member'), 'sub'), parts along dimension 0, may hold values from -6 to 6
- levels: int32 [8], P(('group', 'member')), parts along dimension 0, may hold values from 0 to 17
- enc_w1: bfloat16 [9, 128, 12], replicated, may hold values from -0.625 to 0.625
- enc_b1: float32 [128], replicated, may hold values from -4 to 4
- enc_w2: bfloat16 [9, 128, 128], replicated, may hold values from -0.1875 to 0.1875
- enc_b2: float32 [128], replicated, may hold values from -4 to 4
- den_wa: bfloat16 [9, 128, 256], replicated, may hold values from -0.125 to 0.125
- den_ba: float32 [128], replicated, may hold values from -4 to 4
- noise_gain: float32 [128], replicated, may hold values from -6 to 6
- den_wb: bfloat16 [9, 128, 128], replicated, may hold values from -0.1875 to 0.1875
Outputs:
- denoised: bfloat16 [8, 128, 128, 256], P(('group', 'member'), None, 'strip', 'sub'), parts along dimension 0
The draws below stay inside these ranges and needn't reach their ends.
There are 2 independent parts, one for each index of `group`. The reference program is written for one: setup_inputs(seed, part) draws one part's arguments, and reference() takes and returns one part's arrays. A program takes and returns all parts, laid end to end along the dimension named above; an argument that names none is the same for every part. Nothing has to cross between parts.
All inputs are finite; a program needn't handle non-finite values.
Results may differ from the reference program's by a relative error of at most 0.0043.
The reference program's roundings to bfloat16 on the way (of `enc_first`, `features`, `joined` and `hidden`) count: a program that leaves them out, or rounds other values in their place, can miss the bound.
Values may be sent and summed in bfloat16 or wider, within the bound.
A program may use at most 64 MiB of HBM per device.

```python
import jax
import jax.numpy as jnp
from jax import lax

C = 128
CIN = 12
LEVELS = 18
MEMBERS = 4
H = 128
W = 256


def set_ends(entries, key, low, largest):
    longest = entries.shape.index(max(entries.shape))
    spots = []
    for shift in (0, 1):
        where = [jax.random.randint(jax.random.fold_in(key, axis), (), 0, length) for axis, length in enumerate(entries.shape)]
        where[longest] = (where[longest] + shift) % entries.shape[longest]
        spots.append(tuple(where))
    return entries.at[spots[0]].set(low).at[spots[1]].set(largest)


def block_scale(rng, dims, split, smallest, largest):
    def one(axis_at, blocks):
        heights = jax.random.uniform(jax.random.fold_in(jax.random.fold_in(rng, 6), axis_at), (blocks,), jnp.float32, smallest / len(split), largest / len(split))
        return jnp.repeat(jnp.exp(heights), dims[axis_at] // blocks).reshape((-1,) + (1,) * (len(dims) - axis_at - 1))

    factor_of = one(*split[0])
    for cut in split[1:]:
        factor_of = factor_of * one(*cut)
    return factor_of


def scatter_about(own_key, dims, deviation, bound, pieces=(), held_as=jnp.bfloat16):
    drawn = deviation * jax.random.normal(own_key, dims, jnp.float32)
    if pieces:
        drawn = drawn * block_scale(own_key, dims, pieces, -0.22, 0.18)
    return jnp.clip(drawn, -bound, bound).astype(held_as)


def setup_inputs(seed: int = 0, part: int = 0) -> dict:
    key_list = jax.random.split(jax.random.key(seed), 12)
    part_splits = jax.random.split(jax.random.fold_in(key_list[11], part), 12)
    return {
        "noisy": scatter_about(part_splits[0], (MEMBERS, C, H, W), 1.0, 6.0, ((0, 4), (2, 2), (3, 2))),
        "condition": scatter_about(part_splits[1], (CIN, H, W), 1.0, 6.0, ((1, 8), (2, 2))),
        "levels": set_ends(jax.random.randint(part_splits[2], (MEMBERS,), 0, LEVELS), jax.random.fold_in(part_splits[2], 1), 0, LEVELS - 1).astype(jnp.int32),
        "enc_w1": scatter_about(key_list[3], (9, C, CIN), (9 * CIN) ** -0.5, 0.625),
        "enc_b1": scatter_about(key_list[4], (C,), 1.0, 4.0, (), jnp.float32),
        "enc_w2": scatter_about(key_list[5], (9, C, C), (9 * C) ** -0.5, 0.1875),
        "enc_b2": scatter_about(key_list[6], (C,), 1.0, 4.0, (), jnp.float32),
        "den_wa": scatter_about(key_list[7], (9, C, 2 * C), (18 * C) ** -0.5, 0.125),
        "den_ba": scatter_about(key_list[8], (C,), 1.0, 4.0, (), jnp.float32),
        "noise_gain": scatter_about(key_list[9], (C,), 1.5, 6.0, (), jnp.float32),
        "den_wb": scatter_about(key_list[10], (9, C, C), (9 * C) ** -0.5, 0.1875),
    }


SIGMA_DATA = 0.5
SIG_LOW = 0.25
SIG_HIGH = 4.0

def conv_taps(padded, weight, out_rows, out_cols):
    summed = jnp.zeros((weight.shape[1], out_rows, out_cols), jnp.float32)
    for tap_index in range(9):
        row_shift = tap_index // 3
        col_shift = tap_index % 3
        shifted = padded[:, row_shift:row_shift + out_rows, col_shift:col_shift + out_cols].astype(jnp.float32)
        summed = summed + jnp.einsum('oc,crw->orw', weight[tap_index].astype(jnp.float32), shifted)
    return summed

def pad_cells(field):
    return jnp.pad(field, ((0, 0), (1, 1), (1, 1)))

def reference(noisy, condition, levels, enc_w1, enc_b1, enc_w2, enc_b2, den_wa, den_ba, noise_gain, den_wb):
    enc_first = jax.nn.silu(conv_taps(pad_cells(condition), enc_w1, H, W) + enc_b1[:, None, None]).astype(jnp.bfloat16)
    enc_first = lax.optimization_barrier(enc_first)
    features = (conv_taps(pad_cells(enc_first), enc_w2, H, W) + enc_b2[:, None, None]).astype(jnp.bfloat16)
    features = lax.optimization_barrier(features)

    def one_member(packed):
        member_field, level_index = packed
        noise_sigma = SIG_LOW * (SIG_HIGH / SIG_LOW) ** (level_index.astype(jnp.float32) / (LEVELS - 1))
        spread = noise_sigma * noise_sigma + SIGMA_DATA * SIGMA_DATA
        c_in = 1.0 / jnp.sqrt(spread)
        c_skip = SIGMA_DATA * SIGMA_DATA / spread
        c_out = noise_sigma * SIGMA_DATA / jnp.sqrt(spread)
        c_noise = jnp.log(noise_sigma) / 4.0
        scaled = (c_in * member_field.astype(jnp.float32)).astype(jnp.bfloat16)
        joined = lax.optimization_barrier(jnp.concatenate([scaled, features], axis=0))
        before = conv_taps(pad_cells(joined), den_wa, H, W) + den_ba[:, None, None] + c_noise * noise_gain[:, None, None]
        hidden = lax.optimization_barrier(jax.nn.silu(before).astype(jnp.bfloat16))
        update = conv_taps(pad_cells(hidden), den_wb, H, W)
        return (c_skip * member_field.astype(jnp.float32) + c_out * update).astype(jnp.bfloat16)
    return lax.map(one_member, (noisy, levels))
```

```python
import functools
import math

import jax
import jax.numpy as jnp
from jax import lax
from jax.experimental import pallas as pl
from jax.experimental.pallas import tpu as pltpu
from jax.sharding import PartitionSpec as P

LEVELS = 18
SIGMA_DATA = 0.5
SIG_LOW = 0.25
SIG_HIGH = 4.0
SIDE = 16
SLOT = 16
DEEP = 4
GROUP = 16
MESH = pl.DeviceIdType.MESH
NN = (((1,), (0,)), ((), ()))
TN = (((0,), (0,)), ((), ()))
BF = jnp.bfloat16
F32 = jnp.float32


def largest_part(count, most):
    return max(n for n in range(1, most + 1) if count % n == 0)


def network_kernel(
    members, strips, subs, inputs, levels, noisy_hbm, cond_hbm, w1_hbm, w2_hbm, wa_hbm, wb_hbm,
    b1_hbm, b2_hbm, ba_hbm, gain_hbm, out_hbm,
    noisy_ref, w1_ref, w2_ref, wa_ref, wb_ref, b1_ref, b2_ref, ba_ref, gain_ref,
    cond, cond_own, cond_sib, edge_send, edge_recv, fcol, frow, fcorner,
    n32, w16, lines, first, feats, field, hidden, acc, out_ref, k1, k2, kn, kf, kb,
    load_sem, own_sem, gather_send, gather_recv, cond_send, cond_recv, field_send, field_recv, out_sem,
):
    chans, rows, cols = noisy_ref.shape
    block = cond_hbm.shape[0]
    share = block // inputs
    half = rows // 2
    span = cols + SIDE
    wide = 3 * chans
    member = lax.axis_index("member")
    strip = lax.axis_index("strip")
    sub = lax.axis_index("sub")
    sibling = subs - 1 - sub

    def exists(a):
        return (strip + a >= 0) & (strip + a < strips)

    def beside(a):
        return lax.rem(strip + a + strips, strips)

    loads = {
        name: pltpu.make_async_copy(src, dst, load_sem.at[at])
        for at, (name, src, dst) in enumerate([
            ("noisy", noisy_hbm, noisy_ref), ("w1", w1_hbm, w1_ref), ("w2", w2_hbm, w2_ref),
            ("wa", wa_hbm, wa_ref), ("wb", wb_hbm, wb_ref), ("b1", b1_hbm, b1_ref),
            ("b2", b2_hbm, b2_ref), ("ba", ba_hbm, ba_ref), ("gain", gain_hbm, gain_ref)])
    }
    mine = cond.at[0, pl.ds(pl.multiple_of(member * block, 8), block), :]
    own = pltpu.make_async_copy(cond_hbm, mine, own_sem)

    barrier = pltpu.get_barrier_semaphore()
    for step in range(1, members):
        pl.semaphore_signal(
            barrier, inc=1, device_id={"member": lax.rem(member + step, members)}, device_id_type=MESH)
    pl.semaphore_signal(barrier, inc=1, device_id={"sub": sibling}, device_id_type=MESH)
    for a in (-1, 1):
        for other in (sub, sibling):
            pl.semaphore_signal(
                barrier, inc=1, device_id={"strip": beside(a), "sub": other}, device_id_type=MESH)
    for copy in loads.values():
        copy.start()
    own.start()
    pl.semaphore_wait(barrier, members - 1 + 5)

    gathers = []
    for step in range(1, members):
        copy = pltpu.make_async_remote_copy(
            src_ref=cond_hbm, dst_ref=mine, send_sem=gather_send.at[step], recv_sem=gather_recv.at[step],
            device_id={"member": lax.rem(member + step, members)}, device_id_type=MESH)
        copy.start()
        gathers.append(copy)

    def noise(lanes):
        level = jnp.full((1, lanes), levels[0], jnp.int32).astype(F32)
        sigma = SIG_LOW * jnp.exp(level / (LEVELS - 1) * math.log(SIG_HIGH / SIG_LOW))
        return sigma, sigma * sigma + SIGMA_DATA * SIGMA_DATA

    sigma, spread = noise(chans)
    c_in = 1.0 / jnp.sqrt(spread)
    c_noise = jnp.log(sigma) / 4.0

    def put(dst, pair, spot, b, values):
        base = spot * wide + b * chans
        dst[pair, :values.shape[0], base:base + chans] = values.astype(BF)

    def put_shifted(dst, pair, spot, values):
        size = values.shape[0]
        put(dst, pair, spot, 0, pltpu.roll(values, 1, 0))
        put(dst, pair, spot, 1, values)
        put(dst, pair, spot, 2, pltpu.roll(values, size - 1, 0))

    def loop(count, body):
        def step(at, carry):
            body(at)
            return carry
        lax.fori_loop(0, count, step, 0)

    def own_field(at):
        here = pl.ds(pl.multiple_of(GROUP * at, GROUP), GROUP)
        n32[...] = noisy_ref[:, here, :].astype(F32).reshape(chans * GROUP, cols)
        for r in range(GROUP):
            values = c_in * n32[pl.ds(r, chans, stride=GROUP), :].T
            put_shifted(field, at * (GROUP // 2) + r // 2 + 1, r % 2, values)

    loads["noisy"].wait()
    loop(rows // GROUP, own_field)

    edge_at = pl.multiple_of((1 - sub) * (cols - SIDE), SIDE)
    fields = []

    def send(copies, sems, a, other, src, dst):
        at = len(copies)
        copy = pltpu.make_async_remote_copy(
            src_ref=src, dst_ref=dst, send_sem=sems[0].at[at], recv_sem=sems[1].at[at],
            device_id={"strip": beside(a), "sub": other}, device_id_type=MESH)
        copies.append((copy, a))
        if a == 0:
            copy.start()
        else:
            @pl.when(exists(a))
            def _():
                copy.start()

    def finish(copies):
        for copy, a in copies:
            if a == 0:
                copy.wait()
                continue

            @pl.when(exists(a))
            def _(copy=copy):
                copy.wait_send()

            @pl.when(exists(-a))
            def _(copy=copy):
                copy.wait_recv()

    for spot in range(2):
        lanes = pl.ds(spot * wide + chans, chans)
        send(fields, (field_send, field_recv), 0, sibling,
             field.at[pl.ds(1, half), pl.ds(edge_at, SIDE), lanes], fcol.at[spot])
        for a in (-1, 1):
            pair, end = (1, 1) if a < 0 else (half, 0)
            send(fields, (field_send, field_recv), a, sub,
                 field.at[pair, pl.ds(0, cols), lanes], frow.at[end, spot])
            send(fields, (field_send, field_recv), a, sibling,
                 field.at[pair, pl.ds(edge_at, SIDE), lanes], fcorner.at[end, spot])

    def place(dst, src, start):
        zero = jnp.zeros((wide, chans), BF)
        dst[3 * wide:, :chans] = zero
        dst[:wide, chans:] = zero
        for a in range(3):
            for b in range(3):
                block = src[3 * a + b, :, start:start + chans].astype(F32).T.astype(BF)
                for t in range(2):
                    base = ((a + t) * 3 + b) * chans
                    dst[base:base + chans, t * chans:(t + 1) * chans] = block

    def place_first():
        zero = jnp.zeros((3 * SLOT, chans), BF)
        k1[9 * SLOT:, :chans] = zero
        k1[:3 * SLOT, chans:] = zero
        w16[...] = jnp.zeros(w16.shape, F32)
        for a in range(3):
            for b in range(3):
                w16[3 * a + b, :inputs] = w1_ref[3 * a + b].astype(F32)
                block = w16[3 * a + b].astype(BF)
                for t in range(2):
                    base = ((a + t) * 3 + b) * SLOT
                    k1[base:base + SLOT, t * chans:(t + 1) * chans] = block

    for name in ("w1", "w2", "wa", "wb", "b1", "b2", "ba", "gain"):
        loads[name].wait()
    place(kn, wa_ref, 0)
    place(kf, wa_ref, chans)
    place(k2, w2_ref, 0)
    place(kb, wb_ref, 0)
    place_first()

    def both(value):
        return jnp.concatenate([value, value], axis=1)

    b1 = both(b1_ref[...])
    b2 = both(b2_ref[...])
    ba = both(ba_ref[...] + c_noise * gain_ref[...])

    side_at = lax.broadcasted_iota(jnp.int32, (SIDE, chans), 0)
    in_side = (side_at // (SIDE // 2)) == sub

    def masked(values):
        return jnp.concatenate([values[:cols], jnp.where(in_side, values[cols:], 0.0)], axis=0)

    finish(fields)

    def patch_field(at):
        for q in range(GROUP // 2):
            index = at * (GROUP // 2) + q
            for spot in range(2):
                base = spot * wide + chans
                side = jnp.where(in_side, fcol[spot, index].astype(F32), 0.0)
                low = field[index + 1, 0:SIDE, base:base + chans].astype(F32)
                high = field[index + 1, cols - SIDE:cols, base:base + chans].astype(F32)
                around = jnp.concatenate([high, side, low], axis=0)
                down = pltpu.roll(around, 1, 0).astype(BF)
                up = pltpu.roll(around, 3 * SIDE - 1, 0).astype(BF)
                field[index + 1, cols:, base - chans:base] = down[SIDE:2 * SIDE]
                field[index + 1, 0:SIDE, base - chans:base] = down[2 * SIDE:]
                field[index + 1, cols:, base:base + chans] = side.astype(BF)
                field[index + 1, cols - SIDE:cols, base + chans:base + 2 * chans] = up[:SIDE]
                field[index + 1, cols:, base + chans:base + 2 * chans] = up[SIDE:2 * SIDE]

    loop(rows // GROUP, patch_field)
    for end, a in ((0, -1), (1, 1)):
        for spot in range(2):
            values = jnp.concatenate(
                [frow[end, spot].astype(F32), fcorner[end, spot].astype(F32)], axis=0)
            put_shifted(field, end * (half + 1), spot, masked(jnp.where(exists(a), values, 0.0)))

    def conv(source, weight, pair, count=1, high=span):
        left = source[pl.ds(pair, count), :high].reshape(count * high, 2 * wide)
        right = source[pl.ds(pair + 1, count), :high].reshape(count * high, 2 * wide)
        return lax.dot_general(jnp.concatenate([left, right], axis=1), weight[...], NN,
                               preferred_element_type=F32)

    def stage(count, most, one):
        part = largest_part(count, most)

        def body(at):
            for p in range(part):
                one(at * part + p)
        loop(count // part, body)

    slot_at = lax.broadcasted_iota(jnp.int32, (SLOT, cols), 0)
    lane_at = lax.broadcasted_iota(jnp.int32, (SLOT, cols), 1)
    held_slot = slot_at < inputs
    held_sib = held_slot & (lane_at // (cols - SIDE // 2) == sub) & (
        (lane_at < SIDE // 2) | (lane_at >= cols - SIDE // 2))
    total = members * block

    def cond_row(source, row):
        return source[pl.ds(row // share * block + row % share, SLOT, stride=share), :]

    own.wait()
    for copy in gathers:
        copy.wait()
    cond_own[:total] = cond[0].astype(F32)
    for end in range(2):
        for r in range(DEEP):
            row = r if end == 0 else rows - DEEP + r
            values = jnp.where(held_slot, cond_row(cond_own, row), 0.0)
            edge_send[end, SLOT * r:SLOT * (r + 1)] = values.astype(BF)
    conds = []
    send(conds, (cond_send, cond_recv), 0, sibling, cond.at[0], cond.at[1])
    for a in (-1, 1):
        mine_end, end = (0, 1) if a < 0 else (1, 0)
        send(conds, (cond_send, cond_recv), a, sub, edge_send.at[mine_end], edge_recv.at[0, end])
        send(conds, (cond_send, cond_recv), a, sibling, edge_send.at[mine_end], edge_recv.at[1, end])

    def acc_one(pair):
        acc[pair] = conv(field, kn, pair) + ba

    stage(half + 1, 11, acc_one)

    finish(conds)
    cond_sib[:total] = cond[1].astype(F32)

    def put_line(at, here, there):
        x = jnp.concatenate([here, there], axis=1)
        for b in range(3):
            y = x if b == 1 else pltpu.roll(x, (1 - b) % (2 * cols), 1)
            side = pltpu.roll(y[:, cols:], SIDE * sub, 1)
            lines[at, SLOT * b:SLOT * (b + 1), :cols] = y[:, :cols].astype(BF)
            lines[at, SLOT * b:SLOT * (b + 1), cols:] = side.astype(BF)

    for end, a in ((0, -1), (1, 1)):
        for r in range(DEEP):
            here, there = (
                edge_recv[s, end, SLOT * r:SLOT * (r + 1)].astype(F32) for s in range(2))
            put_line(end * (rows + DEEP) + r, jnp.where(exists(a), here, 0.0),
                     jnp.where(held_sib & exists(a), there, 0.0))

    def line_one(row):
        here = jnp.where(held_slot, cond_row(cond_own, row), 0.0)
        there = jnp.where(held_sib, cond_row(cond_sib, row), 0.0)
        put_line(row + DEEP, here, there)

    stage(rows, 16, line_one)

    def silu(v):
        h = 0.5 * v
        return h * jnp.tanh(h) + h

    def keep(dst, pair, result):
        for spot in range(2):
            put_shifted(dst, pair, spot, masked(result[:, spot * chans:(spot + 1) * chans]))

    def clear(dst, pair, *spots):
        for spot in spots:
            dst[pair, :, spot * wide:(spot + 1) * wide] = jnp.zeros((span, wide), BF)

    def clear_ends(dst, above, below):
        @pl.when(jnp.logical_not(exists(-1)))
        def _():
            for pair, spots in above:
                clear(dst, pair, *spots)

        @pl.when(jnp.logical_not(exists(1)))
        def _():
            for pair, spots in below:
                clear(dst, pair, *spots)

    def first_one(pair):
        left = lines[pl.ds(2 * pair, 4)].reshape(12 * SLOT, 2 * cols)[:, :span]
        result = lax.dot_general(left, k1[...], TN, preferred_element_type=F32)
        keep(first, pair, silu(result + b1))

    stage(half + 3, 7, first_one)
    clear_ends(first, [(0, (0, 1)), (1, (0,))], [(half + 1, (1,)), (half + 2, (0, 1))])

    def feats_one(pair):
        keep(feats, pair, conv(first, k2, pair) + b2)

    stage(half + 2, 17, feats_one)
    clear_ends(feats, [(0, (0, 1))], [(half + 1, (0, 1))])

    def hidden_one(pair):
        keep(hidden, pair, silu(conv(feats, kf, pair) + acc[pair]))

    stage(half + 1, 11, hidden_one)
    clear_ends(hidden, [(0, (0,))], [(half, (1,))])

    sigma_out, spread_out = noise(cols)
    c_skip = (SIGMA_DATA * SIGMA_DATA / spread_out).reshape(1, 1, cols)
    c_out = (sigma_out * SIGMA_DATA / jnp.sqrt(spread_out)).reshape(1, 1, cols)

    def out_copy(at):
        here = pl.ds(pl.multiple_of(GROUP * at, GROUP), GROUP)
        return here, pltpu.make_async_copy(out_ref.at[:, here, :], out_hbm.at[:, here, :], out_sem.at[at])

    def out_group(at):
        for q in range(0, GROUP // 2, 2):
            result = conv(hidden, kb, at * (GROUP // 2) + q, 2, cols)
            for p in range(2):
                for spot in range(2):
                    n32[pl.ds(2 * (q + p) + spot, chans, stride=GROUP), :] = (
                        result[p * cols:(p + 1) * cols, spot * chans:(spot + 1) * chans].T)
        here, copy = out_copy(at)
        update = n32[...].reshape(chans, GROUP, cols)
        out_ref[:, here, :] = (c_skip * noisy_ref[:, here, :].astype(F32) + c_out * update).astype(BF)
        copy.start()

    loop(rows // GROUP, out_group)
    for at in range(rows // GROUP):
        out_copy(at)[1].wait()


def network(members, strips, subs, levels, noisy, cond, inputs, w1, w2, wa, wb, b1, b2, ba, gain):
    chans, rows, cols = noisy.shape
    block = cond.shape[0]
    share = block // inputs
    span = cols + SIDE
    half = rows // 2
    smem = pl.BlockSpec(memory_space=pltpu.SMEM)
    hbm = pl.BlockSpec(memory_space=pl.ANY)
    dma = pltpu.SemaphoreType.DMA

    def held(*shape):
        return pltpu.VMEM(shape, BF)

    def full(*shape):
        return pltpu.VMEM(shape, F32)

    def pairs(count):
        return held(count, span, 6 * chans)

    return pl.pallas_call(
        functools.partial(network_kernel, members, strips, subs, inputs),
        out_shape=jax.ShapeDtypeStruct((chans, rows, cols), BF),
        in_specs=[smem] + [hbm] * 10,
        out_specs=hbm,
        scratch_shapes=[
            held(*noisy.shape), held(*w1.shape), held(*w2.shape), held(*wa.shape), held(*wb.shape),
            full(1, chans), full(1, chans), full(1, chans), full(1, chans),
            held(2, members * block, cols),
            full(members * block + SLOT * share, cols), full(members * block + SLOT * share, cols),
            held(2, DEEP * SLOT, cols), held(2, 2, DEEP * SLOT, cols),
            held(2, half, SIDE, chans), held(2, 2, cols, chans), held(2, 2, SIDE, chans),
            full(chans * GROUP, cols), full(9, SLOT, chans),
            held(rows + 2 * DEEP, 3 * SLOT, 2 * cols),
            pairs(half + 3), pairs(half + 2), pairs(half + 2), pairs(half + 1),
            full(half + 1, span, 2 * chans),
            held(chans, rows, cols),
            held(12 * SLOT, 2 * chans),
        ]
        + [held(12 * chans, 2 * chans)] * 4
        + [dma((9,)), dma, dma((members,)), dma((members,)), dma((5,)), dma((5,)), dma((10,)), dma((10,)),
           dma((rows // GROUP,))],
        compiler_params=pltpu.CompilerParams(
            collective_id=0, has_side_effects=True, vmem_limit_bytes=60 * 1024 * 1024),
        name="network",
    )(levels, noisy, cond, w1, w2, wa, wb, b1, b2, ba, gain)


def local(
    members, strips, subs,
    noisy, condition, levels, enc_w1, enc_b1, enc_w2, enc_b2, den_wa, den_ba, noise_gain, den_wb
):
    inputs, share, width = condition.shape
    out = network(
        members, strips, subs, levels, noisy[0], condition.reshape(inputs * share, width), inputs,
        jnp.transpose(enc_w1, (0, 2, 1)), enc_w2, den_wa, den_wb,
        enc_b1[None], enc_b2[None], den_ba[None], noise_gain[None])
    return out[None]


def solution(mesh):
    return jax.shard_map(
        functools.partial(local, mesh.shape["member"], mesh.shape["strip"], mesh.shape["sub"]),
        mesh=mesh,
        in_specs=(
            P(("group", "member"), None, "strip", "sub"),
            P("group", ("strip", "member"), "sub"),
            P(("group", "member")),
            P(), P(), P(), P(), P(), P(), P(), P(),
        ),
        out_specs=P(("group", "member"), None, "strip", "sub"),
        check_vma=False,
    )
```

```python
import functools
import math

import jax
import jax.numpy as jnp
from jax import lax
from jax.experimental import pallas as pl
from jax.experimental.pallas import tpu as pltpu
from jax.sharding import PartitionSpec as P

LEVELS = 18
SIGMA_DATA = 0.5
SIG_LOW = 0.25
SIG_HIGH = 4.0
SIDE = 16
SLOT = 16
DEEP = 4
GROUP = 16
UNIT = 2
MESH = pl.DeviceIdType.MESH
NN = (((1,), (0,)), ((), ()))
TN = (((0,), (0,)), ((), ()))
BF = jnp.bfloat16
F32 = jnp.float32


def largest_part(count, most):
    return max(n for n in range(1, most + 1) if count % n == 0)


def network_kernel(
    members, strips, subs, inputs, levels, noisy_hbm, cond_hbm, w1_hbm, w2_hbm, wa_hbm, wb_hbm,
    b1_hbm, b2_hbm, ba_hbm, gain_hbm, out_hbm,
    noisy_ref, w1_ref, w2_ref, wa_ref, wb_ref, b1_ref, b2_ref, ba_ref, gain_ref,
    cond, cond_own, cond_sib, edge_send, edge_recv, fcol, frow, fcorner,
    n32, w16, lines, first, feats, field, hidden, acc, out_ref, k1, k2, kn, kf, kb,
    load_sem, noisy_sem, own_sem, gather_send, gather_recv, cond_send, cond_recv, field_send, field_recv, side_send, side_recv, out_sem,
):
    chans, rows, cols = noisy_ref.shape
    block = cond_hbm.shape[0]
    share = block // inputs
    half = rows // 2
    span = cols + SIDE
    wide = 3 * chans
    member = lax.axis_index("member")
    strip = lax.axis_index("strip")
    sub = lax.axis_index("sub")
    sibling = subs - 1 - sub

    def exists(a):
        return (strip + a >= 0) & (strip + a < strips)

    def beside(a):
        return lax.rem(strip + a + strips, strips)

    loads = {
        name: pltpu.make_async_copy(src, dst, load_sem.at[at])
        for at, (name, src, dst) in enumerate([
            ("w1", w1_hbm, w1_ref), ("w2", w2_hbm, w2_ref),
            ("wa", wa_hbm, wa_ref), ("wb", wb_hbm, wb_ref), ("b1", b1_hbm, b1_ref),
            ("b2", b2_hbm, b2_ref), ("ba", ba_hbm, ba_ref), ("gain", gain_hbm, gain_ref)])
    }
    chunks = [
        pltpu.make_async_copy(
            noisy_hbm.at[:, pl.ds(GROUP * at, GROUP), :], noisy_ref.at[:, pl.ds(GROUP * at, GROUP), :],
            noisy_sem.at[at])
        for at in range(rows // GROUP)]
    mine = cond.at[0, pl.ds(pl.multiple_of(member * block, 8), block), :]
    own = pltpu.make_async_copy(cond_hbm, mine, own_sem)

    barrier = pltpu.get_barrier_semaphore()
    for step in range(1, members):
        pl.semaphore_signal(
            barrier, inc=1, device_id={"member": lax.rem(member + step, members)}, device_id_type=MESH)
    pl.semaphore_signal(barrier, inc=1, device_id={"sub": sibling}, device_id_type=MESH)
    for a in (-1, 1):
        for other in (sub, sibling):
            pl.semaphore_signal(
                barrier, inc=1, device_id={"strip": beside(a), "sub": other}, device_id_type=MESH)
    for copy in chunks:
        copy.start()
    own.start()
    for copy in loads.values():
        copy.start()
    pl.semaphore_wait(barrier, members - 1 + 5)

    gathers = []
    for step in range(1, members):
        copy = pltpu.make_async_remote_copy(
            src_ref=cond_hbm, dst_ref=mine, send_sem=gather_send.at[step], recv_sem=gather_recv.at[step],
            device_id={"member": lax.rem(member + step, members)}, device_id_type=MESH)
        copy.start()
        gathers.append(copy)

    def noise(lanes):
        level = jnp.full((1, lanes), levels[0], jnp.int32).astype(F32)
        sigma = SIG_LOW * jnp.exp(level / (LEVELS - 1) * math.log(SIG_HIGH / SIG_LOW))
        return sigma, sigma * sigma + SIGMA_DATA * SIGMA_DATA

    sigma, spread = noise(chans)
    c_in = 1.0 / jnp.sqrt(spread)
    c_noise = jnp.log(sigma) / 4.0

    def put(dst, pair, spot, b, values):
        dst[pair, 3 * spot + b, :values.shape[0]] = values.astype(BF)

    def put_shifted(dst, pair, spot, values):
        size = values.shape[0]
        put(dst, pair, spot, 0, pltpu.roll(values, 1, 0))
        put(dst, pair, spot, 1, values)
        put(dst, pair, spot, 2, pltpu.roll(values, size - 1, 0))

    def loop(count, body):
        def step(at, carry):
            body(at)
            return carry
        lax.fori_loop(0, count, step, 0)

    def own_field(at):
        here = pl.ds(pl.multiple_of(GROUP * at, GROUP), GROUP)
        pltpu.make_async_copy(
            noisy_hbm.at[:, here, :], noisy_ref.at[:, here, :], noisy_sem.at[at]).wait()
        n32[...] = noisy_ref[:, here, :].astype(F32).reshape(chans * GROUP, cols)
        for r in range(GROUP):
            values = c_in * n32[pl.ds(r, chans, stride=GROUP), :].T
            put_shifted(field, at * (GROUP // 2) + r // 2 + 1, r % 2, values)

    loop(rows // GROUP, own_field)

    edge_at = pl.multiple_of((1 - sub) * (cols - SIDE), SIDE)
    fields, sides = [], []

    def plan(copies, sems, a, other, src, dst):
        at = len(copies)
        copy = pltpu.make_async_remote_copy(
            src_ref=src, dst_ref=dst, send_sem=sems[0].at[at], recv_sem=sems[1].at[at],
            device_id={"strip": beside(a), "sub": other}, device_id_type=MESH)
        copies.append((copy, a))

    def launch(copies):
        for copy, a in copies:
            if a == 0:
                copy.start()
                continue

            @pl.when(exists(a))
            def _(copy=copy):
                copy.start()

    def finish(copies):
        for copy, a in copies:
            if a == 0:
                copy.wait()
                continue

            @pl.when(exists(a))
            def _(copy=copy):
                copy.wait_send()

            @pl.when(exists(-a))
            def _(copy=copy):
                copy.wait_recv()

    for spot in range(2):
        at = 3 * spot + 1
        plan(sides, (side_send, side_recv), 0, sibling,
             field.at[pl.ds(1, half), at, pl.ds(edge_at, SIDE), :], fcol.at[spot])
        for a in (-1, 1):
            pair, end = (1, 1) if a < 0 else (half, 0)
            plan(fields, (field_send, field_recv), a, sub,
                 field.at[pair, at, pl.ds(0, cols), :], frow.at[end, spot])
            plan(fields, (field_send, field_recv), a, sibling,
                 field.at[pair, at, pl.ds(edge_at, SIDE), :], fcorner.at[end, spot])

    launch(sides)
    launch(fields)

    def place(dst, src, start):
        zero = jnp.zeros((3, chans, chans), BF)
        dst[0, 9:] = zero
        dst[1, :3] = zero
        for a in range(3):
            for b in range(3):
                block = src[3 * a + b, :, start:start + chans].astype(F32).T.astype(BF)
                for t in range(2):
                    dst[t, (a + t) * 3 + b] = block

    def place_first():
        zero = jnp.zeros((3 * SLOT, chans), BF)
        k1[9 * SLOT:, :chans] = zero
        k1[:3 * SLOT, chans:] = zero
        w16[...] = jnp.zeros(w16.shape, F32)
        for a in range(3):
            for b in range(3):
                w16[3 * a + b, :inputs] = w1_ref[3 * a + b].astype(F32)
                block = w16[3 * a + b].astype(BF)
                for t in range(2):
                    base = ((a + t) * 3 + b) * SLOT
                    k1[base:base + SLOT, t * chans:(t + 1) * chans] = block

    for name in ("w1", "w2", "wa", "wb", "b1", "b2", "ba", "gain"):
        loads[name].wait()
    place(kn, wa_ref, 0)
    place(kf, wa_ref, chans)
    place(k2, w2_ref, 0)
    place(kb, wb_ref, 0)
    place_first()

    def both(value):
        return jnp.concatenate([value, value], axis=1)

    b1 = both(b1_ref[...])
    b2 = both(b2_ref[...])
    ba = both(ba_ref[...] + c_noise * gain_ref[...])

    side_at = lax.broadcasted_iota(jnp.int32, (SIDE, chans), 0)
    in_side = (side_at // (SIDE // 2)) == sub

    def masked(values):
        return jnp.concatenate([values[:cols], jnp.where(in_side, values[cols:], 0.0)], axis=0)

    finish(sides)

    def patch_field(at):
        for q in range(GROUP // 2):
            index = at * (GROUP // 2) + q
            for spot in range(2):
                base = 3 * spot
                side = jnp.where(in_side, fcol[spot, index].astype(F32), 0.0)
                low = field[index + 1, base + 1, 0:SIDE].astype(F32)
                high = field[index + 1, base + 1, cols - SIDE:cols].astype(F32)
                around = jnp.concatenate([high, side, low], axis=0)
                down = pltpu.roll(around, 1, 0).astype(BF)
                up = pltpu.roll(around, 3 * SIDE - 1, 0).astype(BF)
                field[index + 1, base, cols:] = down[SIDE:2 * SIDE]
                field[index + 1, base, 0:SIDE] = down[2 * SIDE:]
                field[index + 1, base + 1, cols:] = side.astype(BF)
                field[index + 1, base + 2, cols - SIDE:cols] = up[:SIDE]
                field[index + 1, base + 2, cols:] = up[SIDE:2 * SIDE]

    loop(rows // GROUP, patch_field)
    def conv(source, weight, pair, count=1, high=span):
        left = jnp.concatenate([
            jnp.concatenate([source[pair + d + k // 6, k % 6, :high] for k in range(12)], axis=1)
            for d in range(count)], axis=0)
        right = jnp.concatenate(
            [weight[t].reshape(12 * chans, chans) for t in range(2)], axis=1)
        return lax.dot_general(left, right, NN, preferred_element_type=F32)

    def stage(count, most, one):
        part = largest_part(count, most)

        def body(at):
            for p in range(part):
                one(at * part + p)
        loop(count // part, body)

    def acc_one(pair):
        acc[pair] = conv(field, kn, pair) + ba

    acc_part = largest_part(half + 1, 11)
    acc_parts = (half + 1) // acc_part

    def acc_body(at):
        for p in range(acc_part):
            acc_one(at * acc_part + p)

    slot_at = lax.broadcasted_iota(jnp.int32, (SLOT, cols), 0)
    lane_at = lax.broadcasted_iota(jnp.int32, (SLOT, cols), 1)
    held_slot = slot_at < inputs
    held_sib = held_slot & (lane_at // (cols - SIDE // 2) == sub) & (
        (lane_at < SIDE // 2) | (lane_at >= cols - SIDE // 2))
    total = members * block

    def cond_row(source, row):
        return source[pl.ds(row // share * block + row % share, SLOT, stride=share), :]

    conds = []
    plan(conds, (cond_send, cond_recv), 0, sibling, cond.at[0], cond.at[1])
    for a in (-1, 1):
        mine_end, end = (0, 1) if a < 0 else (1, 0)
        plan(conds, (cond_send, cond_recv), a, sub, edge_send.at[mine_end], edge_recv.at[0, end])
        plan(conds, (cond_send, cond_recv), a, sibling, edge_send.at[mine_end], edge_recv.at[1, end])

    def halos():
        own.wait()
        for copy in gathers:
            copy.wait()
        cond_own[:total] = cond[0].astype(F32)
        for end in range(2):
            for r in range(DEEP):
                row = r if end == 0 else rows - DEEP + r
                values = jnp.where(held_slot, cond_row(cond_own, row), 0.0)
                edge_send[end, SLOT * r:SLOT * (r + 1)] = values.astype(BF)
        launch(conds)
        finish(fields)
        for end, a in ((0, -1), (1, 1)):
            for spot in range(2):
                values = jnp.concatenate(
                    [frow[end, spot].astype(F32), fcorner[end, spot].astype(F32)], axis=0)
                put_shifted(field, end * (half + 1), spot, masked(jnp.where(exists(a), values, 0.0)))

    early = 1 if acc_parts > 2 else 0

    def acc_step(at):
        @pl.when(at == early)
        def _():
            halos()

        acc_body(lax.rem(at + early, acc_parts))

    loop(acc_parts, acc_step)
    finish(conds)
    cond_sib[:total] = cond[1].astype(F32)

    def put_line(at, here, there):
        x = jnp.concatenate([here, there], axis=1)
        for b in range(3):
            y = x if b == 1 else pltpu.roll(x, (1 - b) % (2 * cols), 1)
            side = jnp.where(sub == 0, y[:, cols:], pltpu.roll(y[:, cols:], SIDE, 1))
            lines[0, at, SLOT * b:SLOT * (b + 1)] = y[:, :cols].astype(BF)
            lines[1, at, SLOT * b:SLOT * (b + 1)] = side.astype(BF)

    for end, a in ((0, -1), (1, 1)):
        for r in range(DEEP):
            here, there = (
                edge_recv[s, end, SLOT * r:SLOT * (r + 1)].astype(F32) for s in range(2))
            put_line(end * (rows + DEEP) + r, jnp.where(exists(a), here, 0.0),
                     jnp.where(held_sib & exists(a), there, 0.0))

    def line_one(row):
        here = jnp.where(held_slot, cond_row(cond_own, row), 0.0)
        there = jnp.where(held_sib, cond_row(cond_sib, row), 0.0)
        put_line(row + DEEP, here, there)

    stage(rows, 16, line_one)

    def silu(v):
        h = 0.5 * v
        return h * jnp.tanh(h) + h

    def keep(dst, pair, result):
        for spot in range(2):
            put_shifted(dst, pair, spot, masked(result[:, spot * chans:(spot + 1) * chans]))

    def clear(dst, pair, *spots):
        for spot in spots:
            dst[pair, 3 * spot:3 * spot + 3] = jnp.zeros((3, span, chans), BF)

    def clear_ends(dst, above, below):
        @pl.when(jnp.logical_not(exists(-1)))
        def _():
            for pair, spots in above:
                clear(dst, pair, *spots)

        @pl.when(jnp.logical_not(exists(1)))
        def _():
            for pair, spots in below:
                clear(dst, pair, *spots)

    def first_one(pair):
        left = jnp.concatenate(
            [lines[h, pl.ds(2 * pair, 4)].reshape(12 * SLOT, cols) for h in range(2)], axis=1)[:, :span]
        result = lax.dot_general(left, k1[...], TN, preferred_element_type=F32)
        keep(first, pair, silu(result + b1))

    stage(half + 3, 7, first_one)
    clear_ends(first, [(0, (0, 1)), (1, (0,))], [(half + 1, (1,)), (half + 2, (0, 1))])

    def feats_one(pair):
        keep(feats, pair, conv(first, k2, pair) + b2)

    stage(half + 2, 17, feats_one)
    clear_ends(feats, [(0, (0, 1))], [(half + 1, (0, 1))])

    def hidden_one(pair):
        keep(hidden, pair, silu(conv(feats, kf, pair) + acc[pair]))

    stage(half + 1, 11, hidden_one)
    clear_ends(hidden, [(0, (0,))], [(half, (1,))])

    sigma_out, spread_out = noise(cols)
    c_skip = (SIGMA_DATA * SIGMA_DATA / spread_out).reshape(1, 1, cols)
    c_out = (sigma_out * SIGMA_DATA / jnp.sqrt(spread_out)).reshape(1, 1, cols)

    def out_copy(at):
        here = pl.ds(pl.multiple_of(GROUP * at, GROUP), GROUP)
        return here, pltpu.make_async_copy(out_ref.at[:, here, :], out_hbm.at[:, here, :], out_sem.at[at])

    def out_group(at):
        for q in range(0, GROUP // 2, UNIT):
            result = conv(hidden, kb, at * (GROUP // 2) + q, UNIT, cols)
            for p in range(UNIT):
                for spot in range(2):
                    n32[pl.ds(2 * (q + p) + spot, chans, stride=GROUP), :] = (
                        result[p * cols:(p + 1) * cols, spot * chans:(spot + 1) * chans].T)
        here, copy = out_copy(at)
        update = n32[...].reshape(chans, GROUP, cols)
        out_ref[:, here, :] = (c_skip * noisy_ref[:, here, :].astype(F32) + c_out * update).astype(BF)
        copy.start()

    loop(rows // GROUP, out_group)
    for at in range(rows // GROUP):
        out_copy(at)[1].wait()


def network(members, strips, subs, levels, noisy, cond, inputs, w1, w2, wa, wb, b1, b2, ba, gain):
    chans, rows, cols = noisy.shape
    block = cond.shape[0]
    share = block // inputs
    span = cols + SIDE
    half = rows // 2
    smem = pl.BlockSpec(memory_space=pltpu.SMEM)
    hbm = pl.BlockSpec(memory_space=pl.ANY)
    dma = pltpu.SemaphoreType.DMA

    def held(*shape):
        return pltpu.VMEM(shape, BF)

    def full(*shape):
        return pltpu.VMEM(shape, F32)

    def pairs(count):
        return held(count, 6, span, chans)

    return pl.pallas_call(
        functools.partial(network_kernel, members, strips, subs, inputs),
        out_shape=jax.ShapeDtypeStruct((chans, rows, cols), BF),
        in_specs=[smem] + [hbm] * 10,
        out_specs=hbm,
        scratch_shapes=[
            held(*noisy.shape), held(*w1.shape), held(*w2.shape), held(*wa.shape), held(*wb.shape),
            full(1, chans), full(1, chans), full(1, chans), full(1, chans),
            held(2, members * block, cols),
            full(members * block + SLOT * share, cols), full(members * block + SLOT * share, cols),
            held(2, DEEP * SLOT, cols), held(2, 2, DEEP * SLOT, cols),
            held(2, half, SIDE, chans), held(2, 2, cols, chans), held(2, 2, SIDE, chans),
            full(chans * GROUP, cols), full(9, SLOT, chans),
            held(2, rows + 2 * DEEP, 3 * SLOT, cols),
            pairs(half + 3), pairs(half + 2), pairs(half + 2), pairs(half + 1),
            full(half + 1, span, 2 * chans),
            held(chans, rows, cols),
            held(12 * SLOT, 2 * chans),
        ]
        + [held(2, 12, chans, chans)] * 4
        + [dma((8,)), dma((rows // GROUP,)), dma, dma((members,)), dma((members,)), dma((5,)), dma((5,)), dma((8,)), dma((8,)), dma((2,)), dma((2,)),
           dma((rows // GROUP,))],
        compiler_params=pltpu.CompilerParams(
            collective_id=0, has_side_effects=True, vmem_limit_bytes=60 * 1024 * 1024),
        name="network",
    )(levels, noisy, cond, w1, w2, wa, wb, b1, b2, ba, gain)


def result_kernel(parts, src, dst, held, read_sem, write_sem):
    size = src.shape[0] // parts

    def copies(source, target, sems):
        return [
            pltpu.make_async_copy(
                source.at[pl.ds(at * size, size)], target.at[pl.ds(at * size, size)], sems.at[at])
            for at in range(parts)]

    reads, writes = copies(src, held, read_sem), copies(held, dst, write_sem)
    for read in reads:
        read.start()
    for read, write in zip(reads, writes):
        read.wait()
        write.start()
    for write in writes:
        write.wait()


def result_of(out):
    parts = largest_part(out.shape[0], 8)
    hbm = pl.BlockSpec(memory_space=pl.ANY)
    dma = pltpu.SemaphoreType.DMA((parts,))
    return pl.pallas_call(
        functools.partial(result_kernel, parts), out_shape=jax.ShapeDtypeStruct(out.shape, out.dtype),
        in_specs=[hbm], out_specs=hbm,
        scratch_shapes=[pltpu.VMEM(out.shape, out.dtype), dma, dma], name="result")(out)


def local(
    members, strips, subs,
    noisy, condition, levels, enc_w1, enc_b1, enc_w2, enc_b2, den_wa, den_ba, noise_gain, den_wb
):
    inputs, share, width = condition.shape
    out = network(
        members, strips, subs, levels, noisy[0], condition.reshape(inputs * share, width), inputs,
        jnp.transpose(enc_w1, (0, 2, 1)), enc_w2, den_wa, den_wb,
        enc_b1[None], enc_b2[None], den_ba[None], noise_gain[None])
    return result_of(out)[None]


def solution(mesh):
    return jax.shard_map(
        functools.partial(local, mesh.shape["member"], mesh.shape["strip"], mesh.shape["sub"]),
        mesh=mesh,
        in_specs=(
            P(("group", "member"), None, "strip", "sub"),
            P("group", ("strip", "member"), "sub"),
            P(("group", "member")),
            P(), P(), P(), P(), P(), P(), P(), P(),
        ),
        out_specs=P(("group", "member"), None, "strip", "sub"),
        check_vma=False,
    )
```

```python
import functools
import math

import jax
import jax.numpy as jnp
from jax import lax
from jax.experimental import pallas as pl
from jax.experimental.pallas import tpu as pltpu
from jax.sharding import PartitionSpec as P

LEVELS = 18
SIGMA_DATA = 0.5
SIG_LOW = 0.25
SIG_HIGH = 4.0
SIDE = 16
SLOT = 16
DEEP = 4
GROUP = 16
UNIT = 2
MESH = pl.DeviceIdType.MESH
NN = (((1,), (0,)), ((), ()))
TN = (((0,), (0,)), ((), ()))
BF = jnp.bfloat16
F32 = jnp.float32


def largest_part(count, most):
    return max(n for n in range(1, most + 1) if count % n == 0)


def network_kernel(
    members, strips, subs, inputs, levels, noisy_hbm, cond_hbm, w1_hbm, w2_hbm, wa_hbm, wb_hbm,
    b1_hbm, b2_hbm, ba_hbm, gain_hbm, out_hbm,
    noisy_ref, w1_ref, w2_ref, wa_ref, wb_ref, b1_ref, b2_ref, ba_ref, gain_ref,
    cond, cond_own, cond_sib, edge_send, edge_recv, fcol, frow, fcorner,
    n32, w16, lines, first, feats, field, hidden, acc, out_ref, k1, k2, kn, kf, kb,
    load_sem, noisy_sem, own_sem, gather_send, gather_recv, cond_send, cond_recv, field_send, field_recv, side_send, side_recv, out_sem,
):
    chans, rows, cols = noisy_ref.shape
    block = cond_hbm.shape[0]
    share = block // inputs
    half = rows // 2
    span = cols + SIDE
    wide = 3 * chans
    member = lax.axis_index("member")
    strip = lax.axis_index("strip")
    sub = lax.axis_index("sub")
    sibling = subs - 1 - sub

    def exists(a):
        return (strip + a >= 0) & (strip + a < strips)

    def beside(a):
        return lax.rem(strip + a + strips, strips)

    loads = {
        name: pltpu.make_async_copy(src, dst, load_sem.at[at])
        for at, (name, src, dst) in enumerate([
            ("w1", w1_hbm, w1_ref), ("w2", w2_hbm, w2_ref),
            ("wa", wa_hbm, wa_ref), ("wb", wb_hbm, wb_ref), ("b1", b1_hbm, b1_ref),
            ("b2", b2_hbm, b2_ref), ("ba", ba_hbm, ba_ref), ("gain", gain_hbm, gain_ref)])
    }
    chunks = [
        pltpu.make_async_copy(
            noisy_hbm.at[:, pl.ds(GROUP * at, GROUP), :], noisy_ref.at[:, pl.ds(GROUP * at, GROUP), :],
            noisy_sem.at[at])
        for at in range(rows // GROUP)]
    mine = cond.at[0, pl.ds(pl.multiple_of(member * block, 8), block), :]
    own = pltpu.make_async_copy(cond_hbm, mine, own_sem)

    barrier = pltpu.get_barrier_semaphore()
    for step in range(1, members):
        pl.semaphore_signal(
            barrier, inc=1, device_id={"member": lax.rem(member + step, members)}, device_id_type=MESH)
    pl.semaphore_signal(barrier, inc=1, device_id={"sub": sibling}, device_id_type=MESH)
    for a in (-1, 1):
        for other in (sub, sibling):
            pl.semaphore_signal(
                barrier, inc=1, device_id={"strip": beside(a), "sub": other}, device_id_type=MESH)
    for copy in chunks:
        copy.start()
    own.start()
    for copy in loads.values():
        copy.start()
    pl.semaphore_wait(barrier, members - 1 + 5)

    gathers = []
    for step in range(1, members):
        copy = pltpu.make_async_remote_copy(
            src_ref=cond_hbm, dst_ref=mine, send_sem=gather_send.at[step], recv_sem=gather_recv.at[step],
            device_id={"member": lax.rem(member + step, members)}, device_id_type=MESH)
        copy.start()
        gathers.append(copy)

    def noise(lanes):
        level = jnp.full((1, lanes), levels[0], jnp.int32).astype(F32)
        sigma = SIG_LOW * jnp.exp(level / (LEVELS - 1) * math.log(SIG_HIGH / SIG_LOW))
        return sigma, sigma * sigma + SIGMA_DATA * SIGMA_DATA

    sigma, spread = noise(chans)
    c_in = 1.0 / jnp.sqrt(spread)
    c_noise = jnp.log(sigma) / 4.0

    def put(dst, pair, spot, b, values):
        dst[pair, 3 * spot + b, :values.shape[0]] = values.astype(BF)

    def put_shifted(dst, pair, spot, values):
        size = values.shape[0]
        put(dst, pair, spot, 0, pltpu.roll(values, 1, 0))
        put(dst, pair, spot, 1, values)
        put(dst, pair, spot, 2, pltpu.roll(values, size - 1, 0))

    def loop(count, body):
        def step(at, carry):
            body(at)
            return carry
        lax.fori_loop(0, count, step, 0)

    def own_field(at):
        here = pl.ds(pl.multiple_of(GROUP * at, GROUP), GROUP)
        pltpu.make_async_copy(
            noisy_hbm.at[:, here, :], noisy_ref.at[:, here, :], noisy_sem.at[at]).wait()
        n32[...] = noisy_ref[:, here, :].astype(F32).reshape(chans * GROUP, cols)
        for r in range(GROUP):
            values = c_in * n32[pl.ds(r, chans, stride=GROUP), :].T
            put_shifted(field, at * (GROUP // 2) + r // 2 + 1, r % 2, values)

    loop(rows // GROUP, own_field)

    edge_at = pl.multiple_of((1 - sub) * (cols - SIDE), SIDE)
    fields, sides = [], []

    def plan(copies, sems, a, other, src, dst):
        at = len(copies)
        copy = pltpu.make_async_remote_copy(
            src_ref=src, dst_ref=dst, send_sem=sems[0].at[at], recv_sem=sems[1].at[at],
            device_id={"strip": beside(a), "sub": other}, device_id_type=MESH)
        copies.append((copy, a))

    def launch(copies):
        for copy, a in copies:
            if a == 0:
                copy.start()
                continue

            @pl.when(exists(a))
            def _(copy=copy):
                copy.start()

    def finish(copies):
        for copy, a in copies:
            if a == 0:
                copy.wait()
                continue

            @pl.when(exists(a))
            def _(copy=copy):
                copy.wait_send()

            @pl.when(exists(-a))
            def _(copy=copy):
                copy.wait_recv()

    for spot in range(2):
        at = 3 * spot + 1
        plan(sides, (side_send, side_recv), 0, sibling,
             field.at[pl.ds(1, half), at, pl.ds(edge_at, SIDE), :], fcol.at[spot])
        for a in (-1, 1):
            pair, end = (1, 1) if a < 0 else (half, 0)
            plan(fields, (field_send, field_recv), a, sub,
                 field.at[pair, at, pl.ds(0, cols), :], frow.at[end, spot])
            plan(fields, (field_send, field_recv), a, sibling,
                 field.at[pair, at, pl.ds(edge_at, SIDE), :], fcorner.at[end, spot])

    launch(sides)
    launch(fields)

    def place(dst, src, start):
        zero = jnp.zeros((3, chans, chans), BF)
        dst[0, 9:] = zero
        dst[1, :3] = zero
        for a in range(3):
            for b in range(3):
                block = src[3 * a + b, :, start:start + chans].astype(F32).T.astype(BF)
                for t in range(2):
                    dst[t, (a + t) * 3 + b] = block

    def place_first():
        zero = jnp.zeros((3 * SLOT, chans), BF)
        k1[9 * SLOT:, :chans] = zero
        k1[:3 * SLOT, chans:] = zero
        w16[...] = jnp.zeros(w16.shape, F32)
        for a in range(3):
            for b in range(3):
                w16[3 * a + b, :inputs] = w1_ref[3 * a + b].astype(F32)
                block = w16[3 * a + b].astype(BF)
                for t in range(2):
                    base = ((a + t) * 3 + b) * SLOT
                    k1[base:base + SLOT, t * chans:(t + 1) * chans] = block

    for name in ("w1", "w2", "wa", "wb", "b1", "b2", "ba", "gain"):
        loads[name].wait()
    place(kn, wa_ref, 0)
    place(kf, wa_ref, chans)
    place(k2, w2_ref, 0)
    place(kb, wb_ref, 0)
    place_first()

    def both(value):
        return jnp.concatenate([value, value], axis=1)

    b1 = both(b1_ref[...])
    b2 = both(b2_ref[...])
    ba = both(ba_ref[...] + c_noise * gain_ref[...])

    side_at = lax.broadcasted_iota(jnp.int32, (SIDE, chans), 0)
    in_side = (side_at // (SIDE // 2)) == sub

    def masked(values):
        return jnp.concatenate([values[:cols], jnp.where(in_side, values[cols:], 0.0)], axis=0)

    finish(sides)

    def patch_field(at):
        for q in range(GROUP // 2):
            index = at * (GROUP // 2) + q
            for spot in range(2):
                base = 3 * spot
                side = jnp.where(in_side, fcol[spot, index].astype(F32), 0.0)
                low = field[index + 1, base + 1, 0:SIDE].astype(F32)
                high = field[index + 1, base + 1, cols - SIDE:cols].astype(F32)
                around = jnp.concatenate([high, side, low], axis=0)
                down = pltpu.roll(around, 1, 0).astype(BF)
                up = pltpu.roll(around, 3 * SIDE - 1, 0).astype(BF)
                field[index + 1, base, cols:] = down[SIDE:2 * SIDE]
                field[index + 1, base, 0:SIDE] = down[2 * SIDE:]
                field[index + 1, base + 1, cols:] = side.astype(BF)
                field[index + 1, base + 2, cols - SIDE:cols] = up[:SIDE]
                field[index + 1, base + 2, cols:] = up[SIDE:2 * SIDE]

    loop(rows // GROUP, patch_field)
    def conv(source, weight, pair, count=1, high=span):
        left = jnp.concatenate([
            jnp.concatenate([source[pair + d + k // 6, k % 6, :high] for k in range(12)], axis=1)
            for d in range(count)], axis=0)
        right = jnp.concatenate(
            [weight[t].reshape(12 * chans, chans) for t in range(2)], axis=1)
        return lax.dot_general(left, right, NN, preferred_element_type=F32)

    def stage(count, most, one):
        part = largest_part(count, most)

        def body(at):
            for p in range(part):
                one(at * part + p)
        loop(count // part, body)

    def acc_one(pair):
        acc[pair] = conv(field, kn, pair) + ba

    acc_part = largest_part(half + 1, 11)
    acc_parts = (half + 1) // acc_part

    def acc_body(at):
        for p in range(acc_part):
            acc_one(at * acc_part + p)

    slot_at = lax.broadcasted_iota(jnp.int32, (SLOT, cols), 0)
    lane_at = lax.broadcasted_iota(jnp.int32, (SLOT, cols), 1)
    held_slot = slot_at < inputs
    held_sib = held_slot & (lane_at // (cols - SIDE // 2) == sub) & (
        (lane_at < SIDE // 2) | (lane_at >= cols - SIDE // 2))
    total = members * block

    def cond_row(source, row):
        return source[pl.ds(row // share * block + row % share, SLOT, stride=share), :]

    conds = []
    plan(conds, (cond_send, cond_recv), 0, sibling, cond.at[0], cond.at[1])
    for a in (-1, 1):
        mine_end, end = (0, 1) if a < 0 else (1, 0)
        plan(conds, (cond_send, cond_recv), a, sub, edge_send.at[mine_end], edge_recv.at[0, end])
        plan(conds, (cond_send, cond_recv), a, sibling, edge_send.at[mine_end], edge_recv.at[1, end])

    def halos():
        own.wait()
        for copy in gathers:
            copy.wait()
        cond_own[:total] = cond[0].astype(F32)
        for end in range(2):
            for r in range(DEEP):
                row = r if end == 0 else rows - DEEP + r
                values = jnp.where(held_slot, cond_row(cond_own, row), 0.0)
                edge_send[end, SLOT * r:SLOT * (r + 1)] = values.astype(BF)
        launch(conds)
        finish(fields)
        for end, a in ((0, -1), (1, 1)):
            for spot in range(2):
                values = jnp.concatenate(
                    [frow[end, spot].astype(F32), fcorner[end, spot].astype(F32)], axis=0)
                put_shifted(field, end * (half + 1), spot, masked(jnp.where(exists(a), values, 0.0)))

    early = 1 if acc_parts > 2 else 0

    def acc_step(at):
        @pl.when(at == early)
        def _():
            halos()

        acc_body(lax.rem(at + early, acc_parts))

    loop(acc_parts, acc_step)
    finish(conds)
    cond_sib[:total] = cond[1].astype(F32)

    def put_line(at, here, there):
        x = jnp.concatenate([here, there], axis=1)
        for b in range(3):
            y = x if b == 1 else pltpu.roll(x, (1 - b) % (2 * cols), 1)
            side = jnp.where(sub == 0, y[:, cols:], pltpu.roll(y[:, cols:], SIDE, 1))
            lines[0, at, SLOT * b:SLOT * (b + 1)] = y[:, :cols].astype(BF)
            lines[1, at, SLOT * b:SLOT * (b + 1)] = side.astype(BF)

    for end, a in ((0, -1), (1, 1)):
        for r in range(DEEP):
            here, there = (
                edge_recv[s, end, SLOT * r:SLOT * (r + 1)].astype(F32) for s in range(2))
            put_line(end * (rows + DEEP) + r, jnp.where(exists(a), here, 0.0),
                     jnp.where(held_sib & exists(a), there, 0.0))

    def line_one(row):
        here = jnp.where(held_slot, cond_row(cond_own, row), 0.0)
        there = jnp.where(held_sib, cond_row(cond_sib, row), 0.0)
        put_line(row + DEEP, here, there)

    stage(rows, 16, line_one)

    def silu(v):
        h = 0.5 * v
        return h * jnp.tanh(h) + h

    def keep(dst, pair, result):
        for spot in range(2):
            put_shifted(dst, pair, spot, masked(result[:, spot * chans:(spot + 1) * chans]))

    def clear(dst, pair, *spots):
        for spot in spots:
            dst[pair, 3 * spot:3 * spot + 3] = jnp.zeros((3, span, chans), BF)

    def clear_ends(dst, above, below):
        @pl.when(jnp.logical_not(exists(-1)))
        def _():
            for pair, spots in above:
                clear(dst, pair, *spots)

        @pl.when(jnp.logical_not(exists(1)))
        def _():
            for pair, spots in below:
                clear(dst, pair, *spots)

    def first_one(pair):
        left = jnp.concatenate(
            [lines[h, pl.ds(2 * pair, 4)].reshape(12 * SLOT, cols) for h in range(2)], axis=1)[:, :span]
        result = lax.dot_general(left, k1[...], TN, preferred_element_type=F32)
        keep(first, pair, silu(result + b1))

    stage(half + 3, 35, first_one)
    clear_ends(first, [(0, (0, 1)), (1, (0,))], [(half + 1, (1,)), (half + 2, (0, 1))])

    def feats_one(pair):
        keep(feats, pair, conv(first, k2, pair) + b2)

    stage(half + 2, 34, feats_one)
    clear_ends(feats, [(0, (0, 1))], [(half + 1, (0, 1))])

    def hidden_one(pair):
        keep(hidden, pair, silu(conv(feats, kf, pair) + acc[pair]))

    stage(half + 1, 33, hidden_one)
    clear_ends(hidden, [(0, (0,))], [(half, (1,))])

    sigma_out, spread_out = noise(cols)
    c_skip = (SIGMA_DATA * SIGMA_DATA / spread_out).reshape(1, 1, cols)
    c_out = (sigma_out * SIGMA_DATA / jnp.sqrt(spread_out)).reshape(1, 1, cols)

    def out_copy(at):
        here = pl.ds(pl.multiple_of(GROUP * at, GROUP), GROUP)
        return here, pltpu.make_async_copy(out_ref.at[:, here, :], out_hbm.at[:, here, :], out_sem.at[at])

    def out_group(at):
        for q in range(0, GROUP // 2, UNIT):
            result = conv(hidden, kb, at * (GROUP // 2) + q, UNIT, cols)
            for p in range(UNIT):
                for spot in range(2):
                    n32[pl.ds(2 * (q + p) + spot, chans, stride=GROUP), :] = (
                        result[p * cols:(p + 1) * cols, spot * chans:(spot + 1) * chans].T)
        here, copy = out_copy(at)
        update = n32[...].reshape(chans, GROUP, cols)
        out_ref[:, here, :] = (c_skip * noisy_ref[:, here, :].astype(F32) + c_out * update).astype(BF)
        copy.start()

    for at in range(rows // GROUP):
        out_group(at)
    for at in range(rows // GROUP):
        out_copy(at)[1].wait()


def network(members, strips, subs, levels, noisy, cond, inputs, w1, w2, wa, wb, b1, b2, ba, gain):
    chans, rows, cols = noisy.shape
    block = cond.shape[0]
    share = block // inputs
    span = cols + SIDE
    half = rows // 2
    smem = pl.BlockSpec(memory_space=pltpu.SMEM)
    hbm = pl.BlockSpec(memory_space=pl.ANY)
    dma = pltpu.SemaphoreType.DMA

    def held(*shape):
        return pltpu.VMEM(shape, BF)

    def full(*shape):
        return pltpu.VMEM(shape, F32)

    def pairs(count):
        return held(count, 6, span, chans)

    return pl.pallas_call(
        functools.partial(network_kernel, members, strips, subs, inputs),
        out_shape=jax.ShapeDtypeStruct((chans, rows, cols), BF),
        in_specs=[smem] + [hbm] * 10,
        out_specs=hbm,
        scratch_shapes=[
            held(*noisy.shape), held(*w1.shape), held(*w2.shape), held(*wa.shape), held(*wb.shape),
            full(1, chans), full(1, chans), full(1, chans), full(1, chans),
            held(2, members * block, cols),
            full(members * block + SLOT * share, cols), full(members * block + SLOT * share, cols),
            held(2, DEEP * SLOT, cols), held(2, 2, DEEP * SLOT, cols),
            held(2, half, SIDE, chans), held(2, 2, cols, chans), held(2, 2, SIDE, chans),
            full(chans * GROUP, cols), full(9, SLOT, chans),
            held(2, rows + 2 * DEEP, 3 * SLOT, cols),
            pairs(half + 3), pairs(half + 2), pairs(half + 2), pairs(half + 1),
            full(half + 1, span, 2 * chans),
            held(chans, rows, cols),
            held(12 * SLOT, 2 * chans),
        ]
        + [held(2, 12, chans, chans)] * 4
        + [dma((8,)), dma((rows // GROUP,)), dma, dma((members,)), dma((members,)), dma((5,)), dma((5,)), dma((8,)), dma((8,)), dma((2,)), dma((2,)),
           dma((rows // GROUP,))],
        compiler_params=pltpu.CompilerParams(
            collective_id=0, has_side_effects=True, vmem_limit_bytes=60 * 1024 * 1024),
        name="network",
    )(levels, noisy, cond, w1, w2, wa, wb, b1, b2, ba, gain)


def result_kernel(parts, src, dst, held, read_sem, write_sem):
    size = src.shape[0] // parts

    def copies(source, target, sems):
        return [
            pltpu.make_async_copy(
                source.at[pl.ds(at * size, size)], target.at[pl.ds(at * size, size)], sems.at[at])
            for at in range(parts)]

    reads, writes = copies(src, held, read_sem), copies(held, dst, write_sem)
    for read in reads:
        read.start()
    for read, write in zip(reads, writes):
        read.wait()
        write.start()
    for write in writes:
        write.wait()


def result_of(out):
    parts = largest_part(out.shape[0], 8)
    hbm = pl.BlockSpec(memory_space=pl.ANY)
    dma = pltpu.SemaphoreType.DMA((parts,))
    return pl.pallas_call(
        functools.partial(result_kernel, parts), out_shape=jax.ShapeDtypeStruct(out.shape, out.dtype),
        in_specs=[hbm], out_specs=hbm,
        scratch_shapes=[pltpu.VMEM(out.shape, out.dtype), dma, dma], name="result")(out)


def local(
    members, strips, subs,
    noisy, condition, levels, enc_w1, enc_b1, enc_w2, enc_b2, den_wa, den_ba, noise_gain, den_wb
):
    inputs, share, width = condition.shape
    out = network(
        members, strips, subs, levels, noisy[0], condition.reshape(inputs * share, width), inputs,
        jnp.transpose(enc_w1, (0, 2, 1)), enc_w2, den_wa, den_wb,
        enc_b1[None], enc_b2[None], den_ba[None], noise_gain[None])
    return result_of(out)[None]


def solution(mesh):
    return jax.shard_map(
        functools.partial(local, mesh.shape["member"], mesh.shape["strip"], mesh.shape["sub"]),
        mesh=mesh,
        in_specs=(
            P(("group", "member"), None, "strip", "sub"),
            P("group", ("strip", "member"), "sub"),
            P(("group", "member")),
            P(), P(), P(), P(), P(), P(), P(), P(),
        ),
        out_specs=P(("group", "member"), None, "strip", "sub"),
        check_vma=False,
    )
```

```python
import functools
import math

import jax
import jax.numpy as jnp
from jax import lax
from jax.experimental import pallas as pl
from jax.experimental.pallas import tpu as pltpu
from jax.sharding import PartitionSpec as P

LEVELS = 18
SIGMA_DATA = 0.5
SIG_LOW = 0.25
SIG_HIGH = 4.0
SIDE = 16
SLOT = 16
DEEP = 4
GROUP = 16
UNIT = 2
MESH = pl.DeviceIdType.MESH
NN = (((1,), (0,)), ((), ()))
TN = (((0,), (0,)), ((), ()))
BF = jnp.bfloat16
F32 = jnp.float32


def largest_part(count, most):
    return max(n for n in range(1, most + 1) if count % n == 0)


def network_kernel(
    members, strips, subs, inputs, levels, noisy_hbm, cond_hbm, w1_hbm, w2_hbm, wa_hbm, wb_hbm,
    b1_hbm, b2_hbm, ba_hbm, gain_hbm, out_hbm,
    noisy_ref, w1_ref, w2_ref, wa_ref, wb_ref, b1_ref, b2_ref, ba_ref, gain_ref,
    cond, cond_own, cond_sib, edge_send, edge_recv, fcol, frow, fcorner,
    n32, w16, lines, first, feats, field, hidden, acc, out_ref, k1, k2, kn, kf, kb,
    load_sem, noisy_sem, own_sem, gather_send, gather_recv, cond_send, cond_recv, field_send, field_recv, side_send, side_recv, out_sem,
):
    chans, rows, cols = noisy_ref.shape
    block = cond_hbm.shape[0]
    share = block // inputs
    half = rows // 2
    span = cols + SIDE
    wide = 3 * chans
    member = lax.axis_index("member")
    strip = lax.axis_index("strip")
    sub = lax.axis_index("sub")
    sibling = subs - 1 - sub

    def exists(a):
        return (strip + a >= 0) & (strip + a < strips)

    def beside(a):
        return lax.rem(strip + a + strips, strips)

    loads = {
        name: pltpu.make_async_copy(src, dst, load_sem.at[at])
        for at, (name, src, dst) in enumerate([
            ("w1", w1_hbm, w1_ref), ("w2", w2_hbm, w2_ref),
            ("wa", wa_hbm, wa_ref), ("wb", wb_hbm, wb_ref), ("b1", b1_hbm, b1_ref),
            ("b2", b2_hbm, b2_ref), ("ba", ba_hbm, ba_ref), ("gain", gain_hbm, gain_ref)])
    }
    chunks = [
        pltpu.make_async_copy(
            noisy_hbm.at[:, pl.ds(GROUP * at, GROUP), :], noisy_ref.at[:, pl.ds(GROUP * at, GROUP), :],
            noisy_sem.at[at])
        for at in range(rows // GROUP)]
    mine = cond.at[0, pl.ds(pl.multiple_of(member * block, 8), block), :]
    own = pltpu.make_async_copy(cond_hbm, mine, own_sem)

    barrier = pltpu.get_barrier_semaphore()
    for step in range(1, members):
        pl.semaphore_signal(
            barrier, inc=1, device_id={"member": lax.rem(member + step, members)}, device_id_type=MESH)
    pl.semaphore_signal(barrier, inc=1, device_id={"sub": sibling}, device_id_type=MESH)
    for a in (-1, 1):
        for other in (sub, sibling):
            pl.semaphore_signal(
                barrier, inc=1, device_id={"strip": beside(a), "sub": other}, device_id_type=MESH)
    for copy in chunks:
        copy.start()
    own.start()
    for copy in loads.values():
        copy.start()
    pl.semaphore_wait(barrier, members - 1 + 5)

    gathers = []
    for step in range(1, members):
        copy = pltpu.make_async_remote_copy(
            src_ref=cond_hbm, dst_ref=mine, send_sem=gather_send.at[step], recv_sem=gather_recv.at[step],
            device_id={"member": lax.rem(member + step, members)}, device_id_type=MESH)
        copy.start()
        gathers.append(copy)

    def noise(lanes):
        level = jnp.full((1, lanes), levels[0], jnp.int32).astype(F32)
        sigma = SIG_LOW * jnp.exp(level / (LEVELS - 1) * math.log(SIG_HIGH / SIG_LOW))
        return sigma, sigma * sigma + SIGMA_DATA * SIGMA_DATA

    sigma, spread = noise(chans)
    c_in = 1.0 / jnp.sqrt(spread)
    c_noise = jnp.log(sigma) / 4.0

    def put(dst, pair, spot, b, values):
        dst[pair, 3 * spot + b, :values.shape[0]] = values.astype(BF)

    def put_shifted(dst, pair, spot, values):
        size = values.shape[0]
        put(dst, pair, spot, 0, pltpu.roll(values, 1, 0))
        put(dst, pair, spot, 1, values)
        put(dst, pair, spot, 2, pltpu.roll(values, size - 1, 0))

    def loop(count, body):
        def step(at, carry):
            body(at)
            return carry
        lax.fori_loop(0, count, step, 0)

    def own_field(at):
        here = pl.ds(pl.multiple_of(GROUP * at, GROUP), GROUP)
        pltpu.make_async_copy(
            noisy_hbm.at[:, here, :], noisy_ref.at[:, here, :], noisy_sem.at[at]).wait()
        n32[...] = noisy_ref[:, here, :].astype(F32).reshape(chans * GROUP, cols)
        for r in range(GROUP):
            values = c_in * n32[pl.ds(r, chans, stride=GROUP), :].T
            put_shifted(field, at * (GROUP // 2) + r // 2 + 1, r % 2, values)

    loop(rows // GROUP, own_field)

    edge_at = pl.multiple_of((1 - sub) * (cols - SIDE), SIDE)
    fields, sides = [], []

    def plan(copies, sems, a, other, src, dst):
        at = len(copies)
        copy = pltpu.make_async_remote_copy(
            src_ref=src, dst_ref=dst, send_sem=sems[0].at[at], recv_sem=sems[1].at[at],
            device_id={"strip": beside(a), "sub": other}, device_id_type=MESH)
        copies.append((copy, a))

    def launch(copies):
        for copy, a in copies:
            if a == 0:
                copy.start()
                continue

            @pl.when(exists(a))
            def _(copy=copy):
                copy.start()

    def finish(copies):
        for copy, a in copies:
            if a == 0:
                copy.wait()
                continue

            @pl.when(exists(a))
            def _(copy=copy):
                copy.wait_send()

            @pl.when(exists(-a))
            def _(copy=copy):
                copy.wait_recv()

    for spot in range(2):
        at = 3 * spot + 1
        plan(sides, (side_send, side_recv), 0, sibling,
             field.at[pl.ds(1, half), at, pl.ds(edge_at, SIDE), :], fcol.at[spot])
        for a in (-1, 1):
            pair, end = (1, 1) if a < 0 else (half, 0)
            plan(fields, (field_send, field_recv), a, sub,
                 field.at[pair, at, pl.ds(0, cols), :], frow.at[end, spot])
            plan(fields, (field_send, field_recv), a, sibling,
                 field.at[pair, at, pl.ds(edge_at, SIDE), :], fcorner.at[end, spot])

    launch(sides)
    launch(fields)

    def place(dst, src, start):
        zero = jnp.zeros((3, chans, chans), BF)
        dst[0, 9:] = zero
        dst[1, :3] = zero
        for a in range(3):
            for b in range(3):
                block = src[3 * a + b, :, start:start + chans].astype(F32).T.astype(BF)
                for t in range(2):
                    dst[t, (a + t) * 3 + b] = block

    def place_first():
        zero = jnp.zeros((3 * SLOT, chans), BF)
        k1[9 * SLOT:, :chans] = zero
        k1[:3 * SLOT, chans:] = zero
        w16[...] = jnp.zeros(w16.shape, F32)
        for a in range(3):
            for b in range(3):
                w16[3 * a + b, :inputs] = w1_ref[3 * a + b].astype(F32)
                block = w16[3 * a + b].astype(BF)
                for t in range(2):
                    base = ((a + t) * 3 + b) * SLOT
                    k1[base:base + SLOT, t * chans:(t + 1) * chans] = block

    for name in ("w1", "w2", "wa", "wb", "b1", "b2", "ba", "gain"):
        loads[name].wait()
    place(kn, wa_ref, 0)
    place(kf, wa_ref, chans)
    place(k2, w2_ref, 0)
    place(kb, wb_ref, 0)
    place_first()

    def both(value):
        return jnp.concatenate([value, value], axis=1)

    b1 = both(b1_ref[...])
    b2 = both(b2_ref[...])
    ba = both(ba_ref[...] + c_noise * gain_ref[...])

    side_at = lax.broadcasted_iota(jnp.int32, (SIDE, chans), 0)
    in_side = (side_at // (SIDE // 2)) == sub

    def masked(values):
        return jnp.concatenate([values[:cols], jnp.where(in_side, values[cols:], 0.0)], axis=0)

    finish(sides)

    def patch_field(at):
        for q in range(GROUP // 2):
            index = at * (GROUP // 2) + q
            for spot in range(2):
                base = 3 * spot
                side = jnp.where(in_side, fcol[spot, index].astype(F32), 0.0)
                low = field[index + 1, base + 1, 0:SIDE].astype(F32)
                high = field[index + 1, base + 1, cols - SIDE:cols].astype(F32)
                around = jnp.concatenate([high, side, low], axis=0)
                down = pltpu.roll(around, 1, 0).astype(BF)
                up = pltpu.roll(around, 3 * SIDE - 1, 0).astype(BF)
                field[index + 1, base, cols:] = down[SIDE:2 * SIDE]
                field[index + 1, base, 0:SIDE] = down[2 * SIDE:]
                field[index + 1, base + 1, cols:] = side.astype(BF)
                field[index + 1, base + 2, cols - SIDE:cols] = up[:SIDE]
                field[index + 1, base + 2, cols:] = up[SIDE:2 * SIDE]

    loop(rows // GROUP, patch_field)
    def conv(source, weight, pair, count=1, high=span):
        left = jnp.concatenate([
            jnp.concatenate([source[pair + d + k // 6, k % 6, :high] for k in range(12)], axis=1)
            for d in range(count)], axis=0)
        right = jnp.concatenate(
            [weight[t].reshape(12 * chans, chans) for t in range(2)], axis=1)
        return lax.dot_general(left, right, NN, preferred_element_type=F32)

    def stage(count, most, one):
        part = largest_part(count, most)

        def body(at):
            for p in range(part):
                one(at * part + p)
        loop(count // part, body)

    def acc_one(pair):
        acc[pair] = conv(field, kn, pair) + ba

    acc_part = largest_part(half + 1, 11)
    acc_parts = (half + 1) // acc_part

    def acc_body(at):
        for p in range(acc_part):
            acc_one(at * acc_part + p)

    slot_at = lax.broadcasted_iota(jnp.int32, (SLOT, cols), 0)
    lane_at = lax.broadcasted_iota(jnp.int32, (SLOT, cols), 1)
    held_slot = slot_at < inputs
    held_sib = held_slot & (lane_at // (cols - SIDE // 2) == sub) & (
        (lane_at < SIDE // 2) | (lane_at >= cols - SIDE // 2))
    total = members * block

    def cond_row(source, row):
        return source[pl.ds(row // share * block + row % share, SLOT, stride=share), :]

    conds = []
    plan(conds, (cond_send, cond_recv), 0, sibling, cond.at[0], cond.at[1])
    for a in (-1, 1):
        mine_end, end = (0, 1) if a < 0 else (1, 0)
        plan(conds, (cond_send, cond_recv), a, sub, edge_send.at[mine_end], edge_recv.at[0, end])
        plan(conds, (cond_send, cond_recv), a, sibling, edge_send.at[mine_end], edge_recv.at[1, end])

    def halos():
        own.wait()
        for copy in gathers:
            copy.wait()
        cond_own[:total] = cond[0].astype(F32)
        for end in range(2):
            for r in range(DEEP):
                row = r if end == 0 else rows - DEEP + r
                values = jnp.where(held_slot, cond_row(cond_own, row), 0.0)
                edge_send[end, SLOT * r:SLOT * (r + 1)] = values.astype(BF)
        launch(conds)
        finish(fields)
        for end, a in ((0, -1), (1, 1)):
            for spot in range(2):
                values = jnp.concatenate(
                    [frow[end, spot].astype(F32), fcorner[end, spot].astype(F32)], axis=0)
                put_shifted(field, end * (half + 1), spot, masked(jnp.where(exists(a), values, 0.0)))

    early = 1 if acc_parts > 2 else 0

    for at in range(acc_parts):
        if at == early:
            halos()
        acc_body((at + early) % acc_parts)
    finish(conds)
    cond_sib[:total] = cond[1].astype(F32)

    def put_line(at, here, there):
        x = jnp.concatenate([here, there], axis=1)
        for b in range(3):
            y = x if b == 1 else pltpu.roll(x, (1 - b) % (2 * cols), 1)
            side = jnp.where(sub == 0, y[:, cols:], pltpu.roll(y[:, cols:], SIDE, 1))
            lines[0, at, SLOT * b:SLOT * (b + 1)] = y[:, :cols].astype(BF)
            lines[1, at, SLOT * b:SLOT * (b + 1)] = side.astype(BF)

    for end, a in ((0, -1), (1, 1)):
        for r in range(DEEP):
            here, there = (
                edge_recv[s, end, SLOT * r:SLOT * (r + 1)].astype(F32) for s in range(2))
            put_line(end * (rows + DEEP) + r, jnp.where(exists(a), here, 0.0),
                     jnp.where(held_sib & exists(a), there, 0.0))

    def line_one(row):
        here = jnp.where(held_slot, cond_row(cond_own, row), 0.0)
        there = jnp.where(held_sib, cond_row(cond_sib, row), 0.0)
        put_line(row + DEEP, here, there)

    stage(rows, 16, line_one)

    def silu(v):
        h = 0.5 * v
        return h * jnp.tanh(h) + h

    def keep(dst, pair, result):
        for spot in range(2):
            put_shifted(dst, pair, spot, masked(result[:, spot * chans:(spot + 1) * chans]))

    def clear(dst, pair, *spots):
        for spot in spots:
            dst[pair, 3 * spot:3 * spot + 3] = jnp.zeros((3, span, chans), BF)

    def clear_ends(dst, above, below):
        @pl.when(jnp.logical_not(exists(-1)))
        def _():
            for pair, spots in above:
                clear(dst, pair, *spots)

        @pl.when(jnp.logical_not(exists(1)))
        def _():
            for pair, spots in below:
                clear(dst, pair, *spots)

    def first_one(pair):
        left = jnp.concatenate(
            [lines[h, pl.ds(2 * pair, 4)].reshape(12 * SLOT, cols) for h in range(2)], axis=1)[:, :span]
        result = lax.dot_general(left, k1[...], TN, preferred_element_type=F32)
        keep(first, pair, silu(result + b1))

    stage(half + 3, 35, first_one)
    clear_ends(first, [(0, (0, 1)), (1, (0,))], [(half + 1, (1,)), (half + 2, (0, 1))])

    def feats_one(pair):
        keep(feats, pair, conv(first, k2, pair) + b2)

    stage(half + 2, 34, feats_one)
    clear_ends(feats, [(0, (0, 1))], [(half + 1, (0, 1))])

    def hidden_one(pair):
        keep(hidden, pair, silu(conv(feats, kf, pair) + acc[pair]))

    stage(half + 1, 33, hidden_one)
    clear_ends(hidden, [(0, (0,))], [(half, (1,))])

    sigma_out, spread_out = noise(cols)
    c_skip = (SIGMA_DATA * SIGMA_DATA / spread_out).reshape(1, 1, cols)
    c_out = (sigma_out * SIGMA_DATA / jnp.sqrt(spread_out)).reshape(1, 1, cols)

    def out_copy(at):
        here = pl.ds(pl.multiple_of(GROUP * at, GROUP), GROUP)
        return here, pltpu.make_async_copy(out_ref.at[:, here, :], out_hbm.at[:, here, :], out_sem.at[at])

    def out_group(at):
        for q in range(0, GROUP // 2, UNIT):
            result = conv(hidden, kb, at * (GROUP // 2) + q, UNIT, cols)
            for p in range(UNIT):
                for spot in range(2):
                    n32[pl.ds(2 * (q + p) + spot, chans, stride=GROUP), :] = (
                        result[p * cols:(p + 1) * cols, spot * chans:(spot + 1) * chans].T)
        here, copy = out_copy(at)
        update = n32[...].reshape(chans, GROUP, cols)
        out_ref[:, here, :] = (c_skip * noisy_ref[:, here, :].astype(F32) + c_out * update).astype(BF)
        copy.start()

    for at in range(rows // GROUP):
        out_group(at)
    for at in range(rows // GROUP):
        out_copy(at)[1].wait()


def network(members, strips, subs, levels, noisy, cond, inputs, w1, w2, wa, wb, b1, b2, ba, gain):
    chans, rows, cols = noisy.shape
    block = cond.shape[0]
    share = block // inputs
    span = cols + SIDE
    half = rows // 2
    smem = pl.BlockSpec(memory_space=pltpu.SMEM)
    hbm = pl.BlockSpec(memory_space=pl.ANY)
    dma = pltpu.SemaphoreType.DMA

    def held(*shape):
        return pltpu.VMEM(shape, BF)

    def full(*shape):
        return pltpu.VMEM(shape, F32)

    def pairs(count):
        return held(count, 6, span, chans)

    return pl.pallas_call(
        functools.partial(network_kernel, members, strips, subs, inputs),
        out_shape=jax.ShapeDtypeStruct((chans, rows, cols), BF),
        in_specs=[smem] + [hbm] * 10,
        out_specs=hbm,
        scratch_shapes=[
            held(*noisy.shape), held(*w1.shape), held(*w2.shape), held(*wa.shape), held(*wb.shape),
            full(1, chans), full(1, chans), full(1, chans), full(1, chans),
            held(2, members * block, cols),
            full(members * block + SLOT * share, cols), full(members * block + SLOT * share, cols),
            held(2, DEEP * SLOT, cols), held(2, 2, DEEP * SLOT, cols),
            held(2, half, SIDE, chans), held(2, 2, cols, chans), held(2, 2, SIDE, chans),
            full(chans * GROUP, cols), full(9, SLOT, chans),
            held(2, rows + 2 * DEEP, 3 * SLOT, cols),
            pairs(half + 3), pairs(half + 2), pairs(half + 2), pairs(half + 1),
            full(half + 1, span, 2 * chans),
            held(chans, rows, cols),
            held(12 * SLOT, 2 * chans),
        ]
        + [held(2, 12, chans, chans)] * 4
        + [dma((8,)), dma((rows // GROUP,)), dma, dma((members,)), dma((members,)), dma((5,)), dma((5,)), dma((8,)), dma((8,)), dma((2,)), dma((2,)),
           dma((rows // GROUP,))],
        compiler_params=pltpu.CompilerParams(
            collective_id=0, has_side_effects=True, vmem_limit_bytes=60 * 1024 * 1024),
        name="network",
    )(levels, noisy, cond, w1, w2, wa, wb, b1, b2, ba, gain)


def result_kernel(parts, src, dst, held, read_sem, write_sem):
    size = src.shape[0] // parts

    def copies(source, target, sems):
        return [
            pltpu.make_async_copy(
                source.at[pl.ds(at * size, size)], target.at[pl.ds(at * size, size)], sems.at[at])
            for at in range(parts)]

    reads, writes = copies(src, held, read_sem), copies(held, dst, write_sem)
    for read in reads:
        read.start()
    for read, write in zip(reads, writes):
        read.wait()
        write.start()
    for write in writes:
        write.wait()


def result_of(out):
    parts = largest_part(out.shape[0], 8)
    hbm = pl.BlockSpec(memory_space=pl.ANY)
    dma = pltpu.SemaphoreType.DMA((parts,))
    return pl.pallas_call(
        functools.partial(result_kernel, parts), out_shape=jax.ShapeDtypeStruct(out.shape, out.dtype),
        in_specs=[hbm], out_specs=hbm,
        scratch_shapes=[pltpu.VMEM(out.shape, out.dtype), dma, dma], name="result")(out)


def local(
    members, strips, subs,
    noisy, condition, levels, enc_w1, enc_b1, enc_w2, enc_b2, den_wa, den_ba, noise_gain, den_wb
):
    inputs, share, width = condition.shape
    out = network(
        members, strips, subs, levels, noisy[0], condition.reshape(inputs * share, width), inputs,
        jnp.transpose(enc_w1, (0, 2, 1)), enc_w2, den_wa, den_wb,
        enc_b1[None], enc_b2[None], den_ba[None], noise_gain[None])
    return result_of(out)[None]


def solution(mesh):
    return jax.shard_map(
        functools.partial(local, mesh.shape["member"], mesh.shape["strip"], mesh.shape["sub"]),
        mesh=mesh,
        in_specs=(
            P(("group", "member"), None, "strip", "sub"),
            P("group", ("strip", "member"), "sub"),
            P(("group", "member")),
            P(), P(), P(), P(), P(), P(), P(), P(),
        ),
        out_specs=P(("group", "member"), None, "strip", "sub"),
        check_vma=False,
    )
```
